32 devices in a mesh: layout: 4 (over z), gx: 4 (over y, core), gy: 2 (over x).
Axes of the slice: x: 2, y: 2, z: 4, core: 2. Of those that a mesh axis runs over, the one named last changes fastest.
Arguments:
- state: float32 [4, 4, 64, 32, 256], P('layout', None, 'gx', None, 'gy'), may hold values from -2 to 2
- planes: float32 [8, 4, 32, 256], P('layout', None, None, 'gy'), may hold values from -2 to 2
- turbine_cell: int32 [4, 64, 32, 256], P('layout', 'gx', None, 'gy'), may hold values from -1 to 15, as said below
- active: int32 [4, 16], P('layout'), may hold values 0 or 1
- yaw_sector: int32 [4, 16], P('layout'), may hold values from 0 to 7
- slot: int32 [4], replicated, may hold values from 0 to 7
Outputs:
- fields: float32 [4, 4, 64, 32, 256], P('layout', None, 'gx', None, 'gy')
The draws below stay inside these ranges and needn't reach their ends.
Inputs may be any that keep to these rules, and one draw needn't show every extreme that they name: `turbine_cell`: cells of value t form turbine t's actuator disk: one streamwise cell, 11 levels around level 16 and 11 spanwise cells (periodic). Every turbine has its disk and disks don't intersect; -1 elsewhere.
All inputs are finite; a program needn't handle non-finite values. No bound on the sum of `active` on one device may be relied on, other than what follows from the above.
Results may differ from the reference program's by a relative error of at most 0.00015.
Values sent between devices are 32-bit elements; how exact they have to be, the bound alone decides.
A program may use at most 64 MiB of HBM per device.

```python
import math
import jax
import jax.numpy as jnp
from jax import lax

NZ = 32
STEPS = 4
SWEEPS = 4
RADIUS = 5
TSPACE = 32
NLAY = 4
NX = 64
NY = 256
TURB = 16
PLANES = 8


def ripple(index, phase):
    return jnp.sin((index + phase).astype(jnp.float32) * (0.5 * math.pi))


def jitter_field(key, extent):
    return jnp.clip(0.3 * jax.random.normal(key, extent, jnp.float32), -0.55, 0.55)


def draw_state(key, part):
    jitter = jitter_field(jax.random.fold_in(key, 101), (NLAY, 4, NX, NZ, NY))
    phases = jax.random.randint(jax.random.fold_in(key, 103), (3, NLAY), 0, 4)
    stream = jnp.arange(NX, dtype=jnp.int32)[None, :, None, None]
    levels = jnp.arange(NZ, dtype=jnp.int32)[None, None, :, None]
    spanwise = jnp.arange(NY, dtype=jnp.int32)[None, None, None, :]
    phase_x = phases[0][:, None, None, None]
    phase_z = phases[1][:, None, None, None]
    phase_y = phases[2][:, None, None, None]
    stream_wind = jitter[:, 0] + 1.4 * ripple(stream, phase_x)
    span_wind = jitter[:, 1] + 1.4 * ripple(spanwise, phase_y)
    vertical_wind = jitter[:, 2] + 0.5 * ripple(levels, phase_z)
    warmth = jitter[:, 3] + 0.6 * ripple(stream + 1, phase_x)
    fields = jnp.stack([stream_wind, span_wind, vertical_wind, warmth], axis=1)
    return jnp.clip(fields, -1.98, 1.98)


def draw_planes(key, part):
    jitter = jitter_field(jax.random.fold_in(key, 201), (PLANES, 4, NZ, NY))
    phases = jax.random.randint(jax.random.fold_in(key, 203), (2, PLANES), 0, 4)
    spanwise = jnp.arange(NY, dtype=jnp.int32)[None, None, :]
    phase_u = phases[0][:, None, None]
    phase_v = phases[1][:, None, None]
    stream_wind = jitter[:, 0] + 0.8 * ripple(spanwise, phase_u)
    span_wind = jitter[:, 1] + 1.4 * ripple(spanwise, phase_v)
    vertical_wind = jitter[:, 2]
    warmth = jitter[:, 3]
    fields = jnp.stack([stream_wind, span_wind, vertical_wind, warmth], axis=1)
    return jnp.clip(fields, -1.98, 1.98)


def draw_turbine_cell(key, part):
    blocks_x = NX // TSPACE
    blocks_y = NY // TSPACE
    key_x = jax.random.fold_in(key, 11)
    key_y = jax.random.fold_in(key, 23)
    offset_x = jax.random.randint(key_x, (NLAY, blocks_x * blocks_y), 0, TSPACE)
    offset_y = jax.random.randint(key_y, (NLAY, blocks_x * blocks_y), RADIUS - TSPACE // 2, TSPACE // 2 - RADIUS)
    stream = jnp.arange(NX)
    span = jnp.arange(NY)
    levels = jnp.arange(NZ)
    block_x = stream // TSPACE
    block_y = (span + TSPACE // 2) // TSPACE % blocks_y
    inside_y = (span + TSPACE // 2) % TSPACE - TSPACE // 2
    turbine = block_x[:, None] * blocks_y + block_y[None, :]
    chosen_x = jnp.take(offset_x, turbine, axis=1)
    chosen_y = jnp.take(offset_y, turbine, axis=1)
    hit = (stream[None, :, None] % TSPACE == chosen_x) & (jnp.abs(inside_y[None, None, :] - chosen_y) <= RADIUS)
    level_hit = jnp.abs(levels - NZ // 2) <= RADIUS
    both = hit[:, :, None, :] & level_hit[None, None, :, None]
    return jnp.where(both, turbine[None, :, None, :], -1).astype(jnp.int32)


def place_ends(values, stream_key, low, largest):
    shape = values.shape
    place = [jax.random.randint(jax.random.fold_in(stream_key, axis), (), 0, shape[axis]) for axis in range(len(shape))]
    values = values.at[tuple(place)].set(low)
    longest = shape.index(max(shape))
    place[longest] = (place[longest] + 1) % shape[longest]
    return values.at[tuple(place)].set(largest)


def setup_inputs(seed: int = 0) -> dict:
    arg_keys = jax.random.split(jax.random.key(seed), 7)
    state = draw_state(jax.random.fold_in(arg_keys[6], 71), 0)
    planes = draw_planes(jax.random.fold_in(arg_keys[6], 71), 0)
    turbine_cell = draw_turbine_cell(jax.random.fold_in(arg_keys[6], 71), 0)
    active = place_ends((jax.random.randint(arg_keys[3], (NLAY, TURB), 0, 4) < 3).astype(jnp.int32), jax.random.fold_in(arg_keys[3], 1), 0, 1)
    yaw_sector = place_ends(jax.random.randint(arg_keys[4], (NLAY, TURB), 0, 8), jax.random.fold_in(arg_keys[4], 1), 0, 7).astype(jnp.int32)
    slot = place_ends(jax.random.randint(arg_keys[5], (STEPS,), 0, PLANES), jax.random.fold_in(arg_keys[5], 1), 0, PLANES - 1).astype(jnp.int32)
    return dict(state=state, planes=planes, turbine_cell=turbine_cell, active=active, yaw_sector=yaw_sector, slot=slot)


TIME_STEP = 0.25
VISCOSITY = 0.02
SMAGORINSKY = 0.0289
DIFFUSIVITY_RATIO = 1.0 / 0.7
BUOYANCY = 0.5
THRUST_COEFF = 1.33
YAW_INCREMENT = 0.1

def profiles(levels):
    height = (jnp.arange(levels).astype(jnp.float32) + 0.5) / levels
    wind_speed = height ** (1.0 / 7.0)
    warmth = 0.5 * height
    zeros = jnp.zeros((levels,), jnp.float32)
    return jnp.stack([wind_speed, zeros, zeros, warmth])

def pad_levels(values):
    keeping = jnp.array([1.0, 1.0, 0.0, 1.0], jnp.float32).reshape(4, 1, 1, 1)
    return jnp.concatenate([values[:, :, :1] * keeping, values, values[:, :, -1:] * keeping], axis=2)

def stencil(padded):
    centre = padded[:, 1:-1, 1:-1, 1:-1]
    along_x = (padded[:, 2:, 1:-1, 1:-1] - padded[:, :-2, 1:-1, 1:-1]) * 0.5
    along_z = (padded[:, 1:-1, 2:, 1:-1] - padded[:, 1:-1, :-2, 1:-1]) * 0.5
    along_y = (padded[:, 1:-1, 1:-1, 2:] - padded[:, 1:-1, 1:-1, :-2]) * 0.5
    laplacian = padded[:, 2:, 1:-1, 1:-1] + padded[:, :-2, 1:-1, 1:-1] + padded[:, 1:-1, 2:, 1:-1] + padded[:, 1:-1, :-2, 1:-1] + padded[:, 1:-1, 1:-1, 2:] + padded[:, 1:-1, 1:-1, :-2] - 6.0 * centre
    return (centre, along_x, along_y, along_z, laplacian)

def tendency(padded, mean_theta, force_u, force_v):
    centre, along_x, along_y, along_z, laplacian = stencil(padded)
    advect = centre[0] * along_x + centre[1] * along_y + centre[2] * along_z
    shear_xy = 0.5 * (along_y[0] + along_x[1])
    shear_xz = 0.5 * (along_z[0] + along_x[2])
    shear_yz = 0.5 * (along_z[1] + along_y[2])
    strain = jnp.sqrt(2.0 * (along_x[0] ** 2 + along_y[1] ** 2 + along_z[2] ** 2) + 4.0 * (shear_xy ** 2 + shear_xz ** 2 + shear_yz ** 2))
    viscous = VISCOSITY + SMAGORINSKY * strain
    scaling = jnp.array([1.0, 1.0, 1.0, DIFFUSIVITY_RATIO], jnp.float32).reshape(4, 1, 1, 1)
    extra = jnp.stack([force_u, force_v, BUOYANCY * (centre[3] - mean_theta[None, :, None]), jnp.zeros_like(force_u)])
    return (centre, laplacian * viscous * scaling - advect + extra)

def disk_terms(values, disk_ids, yaw_angle):
    turbines = yaw_angle.shape[0]
    slot_ids = disk_ids + 1
    cos_cell = jnp.take(jnp.concatenate([jnp.zeros((1,), jnp.float32), jnp.cos(yaw_angle)]), slot_ids)
    sin_cell = jnp.take(jnp.concatenate([jnp.zeros((1,), jnp.float32), jnp.sin(yaw_angle)]), slot_ids)
    normal = values[0] * cos_cell + values[1] * sin_cell
    disk_sums = jax.ops.segment_sum(normal.reshape(-1), slot_ids.reshape(-1), num_segments=turbines + 1)[1:]
    return (cos_cell, sin_cell, disk_sums)

def disk_force(disk_sums, running, disk_ids, cos_cell, sin_cell):
    disk_speed = disk_sums / float((2 * RADIUS + 1) ** 2)
    thrust = -0.5 * THRUST_COEFF * disk_speed * jnp.abs(disk_speed) * running
    per_cell = jnp.take(jnp.concatenate([jnp.zeros((1,), jnp.float32), thrust]), disk_ids + 1)
    return (per_cell * cos_cell, per_cell * sin_cell)

def divergence(extended):
    vertical = extended[2][1:-1, :, 1:-1]
    zeros = jnp.zeros_like(vertical[:, :1])
    padded_w = jnp.concatenate([zeros, vertical, zeros], axis=1)
    return (extended[0][2:, :, 1:-1] - extended[0][:-2, :, 1:-1]) * 0.5 + (extended[1][1:-1, :, 2:] - extended[1][1:-1, :, :-2]) * 0.5 + (padded_w[:, 2:] - padded_w[:, :-2]) * 0.5

def vertical_pair(padded):
    centre = padded[1:-1, :, 1:-1]
    upward = jnp.concatenate([centre[:, 1:], centre[:, -1:]], axis=1)
    downward = jnp.concatenate([centre[:, :1], centre[:, :-1]], axis=1)
    return (upward, downward)

def jacobi(padded, source):
    upward, downward = vertical_pair(padded)
    beside_all = padded[2:, :, 1:-1] + padded[:-2, :, 1:-1] + padded[1:-1, :, 2:] + padded[1:-1, :, :-2] + upward + downward
    return (beside_all - source) / 6.0

def gradient(padded):
    upward, downward = vertical_pair(padded)
    return jnp.stack([(padded[2:, :, 1:-1] - padded[:-2, :, 1:-1]) * 0.5, (padded[1:-1, :, 2:] - padded[1:-1, :, :-2]) * 0.5, (upward - downward) * 0.5])

def wrap_span(values):
    return jnp.concatenate([values[..., -1:], values, values[..., :1]], axis=-1)

def pad_pressure(pressure):
    zeros = jnp.zeros_like(pressure[:1])
    return wrap_span(jnp.concatenate([zeros, pressure, zeros], axis=0))

def advance(fields, inflow, disk_ids, yaw_angle, running):
    theta_sum = lax.optimization_barrier(jnp.sum(fields[3], axis=(0, 2)))
    cos_cell, sin_cell, disk_sums = disk_terms(fields, disk_ids, yaw_angle)
    cell_count = fields.shape[1] * fields.shape[3]
    extended = wrap_span(jnp.concatenate([inflow[:, None], fields, fields[:, -1:]], axis=1))
    force_u, force_v = disk_force(disk_sums, running, disk_ids, cos_cell, sin_cell)
    current, tendencies = tendency(pad_levels(extended), theta_sum / cell_count, force_u, force_v)
    stepped = current + TIME_STEP * tendencies
    provisional = stepped[:3]
    star_ext = wrap_span(jnp.concatenate([inflow[:3, None], provisional, provisional[:, -1:]], axis=1))
    source = divergence(star_ext)
    pressure = -source / 6.0
    for sweep_index in range(SWEEPS):
        pressure = jacobi(pad_pressure(pressure), source)
    gradients = gradient(pad_pressure(pressure))
    return jnp.concatenate([provisional - gradients, stepped[3:]], axis=0)

def reference(state, planes, turbine_cell, active, yaw_sector, slot):
    mean_wind = profiles(state.shape[3])

    def evolve_layout(items):
        start_fields, disk_ids, running, sectors = items
        fields = start_fields + mean_wind[:, None, :, None]
        yaw_angle = (sectors.astype(jnp.float32) - 3.5) * YAW_INCREMENT
        running_f = running.astype(jnp.float32)
        for step_index in range(STEPS):
            inflow = lax.dynamic_index_in_dim(planes, slot[step_index], 0, keepdims=False) + mean_wind[:, :, None]
            fields = advance(fields, inflow, disk_ids, yaw_angle, running_f)
        return fields
    return lax.map(evolve_layout, (state, turbine_cell, active, yaw_sector))
```

```python
import functools

import jax
import jax.numpy as jnp
from jax import lax
from jax.experimental import pallas as pl
from jax.experimental.pallas import tpu as pltpu
from jax.sharding import PartitionSpec as P

STEPS = 4
SWEEPS = 4
RADIUS = 5

TIME_STEP = 0.25
VISCOSITY = 0.02
SMAGORINSKY = 0.0289
DIFFUSIVITY_RATIO = 1.0 / 0.7
BUOYANCY = 0.5
THRUST_COEFF = 1.33
YAW_INCREMENT = 0.1
MESH = pl.DeviceIdType.MESH


def profiles(levels):
    height = (jnp.arange(levels).astype(jnp.float32) + 0.5) / levels
    return jnp.stack([height ** (1.0 / 7.0), 0.5 * height])


def kernel(
    NL, GX, L, R, K, H, turbines, held, columns,
    slot, table, prof, ids, state, planes,
    out,
    F, G, U, RR, PP, PL, ID, SU, FO, TS,
    e_s, e_r, i_s, i_r, p_s, p_r, a_s, a_r, b_s, b_r, c_s, c_r, t_s, t_r, o_s, o_r, loc,
):
    lay = lax.axis_index("layout")
    gx = lax.axis_index("gx")
    gy = lax.axis_index("gy")
    N = GX * L

    def turned(g, q):
        odd = lax.rem(g, 2)
        return q + odd * (L - 1 - 2 * q)

    s = gx * L + turned(gx, gy)
    first = s == 0
    last = s == N - 1

    def device_of(t):
        g = t // L
        return {"gx": g, "gy": turned(g, lax.rem(t, L))}

    right = device_of(lax.rem(s + 1, N))
    left = device_of(lax.rem(s + N - 1, N))

    barrier = pltpu.get_barrier_semaphore()
    for d in range(1, N):
        pl.semaphore_signal(barrier, inc=1, device_id=device_of(lax.rem(s + d, N)), device_id_type=MESH)

    @pl.when(gx == 0)
    def _():
        for d in range(1, NL):
            for j in range(L):
                pl.semaphore_signal(
                    barrier, inc=1,
                    device_id={"layout": lax.rem(lay + d, NL), "gx": 0, "gy": j},
                    device_id_type=MESH,
                )

    q_me = turned(gx, gy)
    own_state = pltpu.make_async_copy(
        state.at[0, :, pl.ds(q_me * R, R)], F.at[:, pl.ds(1, R), gy], loc.at[0]
    )
    own_ids = pltpu.make_async_copy(ids.at[q_me], ID.at[gy], loc.at[1])
    own_state.start()
    own_ids.start()
    own_planes = pltpu.make_async_copy(
        planes, PL.at[pl.ds(lay * held, held), :, gy], loc.at[2]
    )

    @pl.when(first)
    def _():
        own_planes.start()

    zero = jnp.zeros((L, K, 128), jnp.float32)
    for buf in [RR] + [PP.at[i] for i in range(SWEEPS)]:
        @pl.when(first)
        def _():
            def body(i, c):
                buf[i] = zero
                return c
            lax.fori_loop(0, H, body, 0)

        @pl.when(last)
        def _():
            def body(i, c):
                buf[R + H + i] = zero
                return c
            lax.fori_loop(0, H, body, 0)

    pl.semaphore_wait(barrier, N - 1 + jnp.where(gx == 0, (NL - 1) * L, 0))

    def ids_copy(d):
        peer = lax.rem(gy + d, L)
        return pltpu.make_async_remote_copy(
            src_ref=ids.at[turned(gx, peer)], dst_ref=ID.at[gy],
            send_sem=i_s.at[d], recv_sem=i_r.at[d],
            device_id={"gy": peer}, device_id_type=MESH,
        )

    def ids_landing(d):
        return pltpu.make_async_remote_copy(
            src_ref=ids.at[q_me], dst_ref=ID.at[lax.rem(gy + L - d, L)],
            send_sem=i_s.at[d], recv_sem=i_r.at[d],
            device_id={"gy": lax.rem(gy + L - d, L)}, device_id_type=MESH,
        )

    def state_copy(d):
        peer = lax.rem(gy + d, L)
        return pltpu.make_async_remote_copy(
            src_ref=state.at[0, :, pl.ds(turned(gx, peer) * R, R)],
            dst_ref=F.at[:, pl.ds(1, R), gy],
            send_sem=e_s.at[d], recv_sem=e_r.at[d],
            device_id={"gy": peer}, device_id_type=MESH,
        )

    def state_landing(d):
        peer = lax.rem(gy + L - d, L)
        return pltpu.make_async_remote_copy(
            src_ref=state.at[0, :, pl.ds(q_me * R, R)],
            dst_ref=F.at[:, pl.ds(1, R), peer],
            send_sem=e_s.at[d], recv_sem=e_r.at[d],
            device_id={"gy": peer}, device_id_type=MESH,
        )

    def planes_copy(d):
        return pltpu.make_async_remote_copy(
            src_ref=planes, dst_ref=PL.at[pl.ds(lay * held, held), :, gy],
            send_sem=p_s.at[d], recv_sem=p_r.at[d, gy],
            device_id={"layout": lax.rem(lay + d, NL), "gx": 0, "gy": 0},
            device_id_type=MESH,
        )

    def planes_landing(d, j):
        source = lax.rem(lay + NL - d, NL)
        return pltpu.make_async_remote_copy(
            src_ref=planes, dst_ref=PL.at[pl.ds(source * held, held), :, j],
            send_sem=p_s.at[d], recv_sem=p_r.at[d, j],
            device_id={"layout": source, "gx": 0, "gy": j},
            device_id_type=MESH,
        )

    for d in range(1, L):
        ids_copy(d).start()
        state_copy(d).start()

    @pl.when(gx == 0)
    def _():
        for d in range(1, NL):
            planes_copy(d).start()

        @pl.when(gy != 0)
        def _():
            planes_copy(0).start()

    own_ids.wait()
    for d in range(1, L):
        ids_copy(d).wait_send()
        ids_landing(d).wait_recv()

    lane = lax.broadcasted_iota(jnp.int32, (K, 128), 1)
    level = lax.broadcasted_iota(jnp.int32, (K, 128), 0)
    at_first, at_last = lane == 0, lane == 127
    at_floor, at_top = level == 0, level == K - 1
    low = K // 2 - RADIUS
    in_band = (level >= low) & (level <= low + 2 * RADIUS)

    def beside_y(tiles, l):
        f = tiles[l]
        before = pltpu.roll(jnp.where(at_last, tiles[(l - 1) % L], f), 1, 1)
        after = pltpu.roll(jnp.where(at_first, tiles[(l + 1) % L], f), 127, 1)
        return before, after

    def beside_k(f, keep=True):
        edge = f if keep else jnp.zeros_like(f)
        below = jnp.where(at_floor, edge, pltpu.roll(f, 1, 0))
        above = jnp.where(at_top, edge, pltpu.roll(f, K - 1, 0))
        return below, above

    ID_all = [ID[l] for l in range(L)]
    cosines = [jnp.zeros((R, 128), jnp.float32) for l in range(L)]
    sines = [jnp.zeros((R, 128), jnp.float32) for l in range(L)]
    runs = [jnp.zeros((R, 128), jnp.float32) for l in range(L)]
    for t in range(turbines):
        for l in range(L):
            here = ID_all[l] == t
            cosines[l] = jnp.where(here, table[0, t], cosines[l])
            sines[l] = jnp.where(here, table[1, t], sines[l])
            runs[l] = jnp.where(here, table[2, t], runs[l])
    for l in range(L):
        FO[2, l] = cosines[l]
        FO[3, l] = sines[l]
        FO[4, l] = runs[l]

    def disk_forces():
        lane_r = lax.broadcasted_iota(jnp.int32, (R, 128), 1)
        names = [ID[l] for l in range(L)]
        normal = [SU[0, l] * FO[2, l] + SU[1, l] * FO[3, l] for l in range(L)]
        for l in range(L):
            total = normal[l]
            for shift in range(1, 2 * RADIUS + 1):
                for towards in (-1, 1):
                    other = (l - towards) % L
                    amount = shift if towards == 1 else 128 - shift
                    wraps = (lane_r >= 128 - shift) if towards == 1 else (lane_r < shift)
                    n_sh = pltpu.roll(jnp.where(wraps, normal[other], normal[l]), amount, 1)
                    i_sh = pltpu.roll(jnp.where(wraps, names[other], names[l]), amount, 1)
                    total = total + jnp.where(i_sh == names[l], n_sh, 0.0)
            speed = total / float((2 * RADIUS + 1) ** 2)
            thrust = -0.5 * THRUST_COEFF * speed * jnp.abs(speed) * FO[4, l]
            FO[0, l] = thrust * FO[2, l]
            FO[1, l] = thrust * FO[3, l]

    def disk_sums(row, l, u, v):
        SU[0, l, pl.ds(row, 1), :] = jnp.sum(jnp.where(in_band, u, 0.0), axis=0, keepdims=True)
        SU[1, l, pl.ds(row, 1), :] = jnp.sum(jnp.where(in_band, v, 0.0), axis=0, keepdims=True)

    groups = K // 8
    width = 128 // groups
    lane_8 = lax.broadcasted_iota(jnp.int32, (8, 128), 1)

    def theta_copy(par, d):
        return pltpu.make_async_remote_copy(
            src_ref=TS.at[par, 0], dst_ref=TS.at[par, d],
            send_sem=t_s.at[par, d], recv_sem=t_r.at[par, d],
            device_id=device_of(lax.rem(s + d, N)), device_id_type=MESH,
        )

    def send_theta(par, total):
        packed = jnp.zeros((8, 128), jnp.float32)
        for g in range(groups):
            part = jnp.sum(total[g * 8:(g + 1) * 8], axis=1, keepdims=True)
            packed = jnp.where(lane_8 // width == g, part, packed)
        TS[par, 0] = packed
        for d in range(1, N):
            theta_copy(par, d).start()

    def mean_theta(par):
        for d in range(1, N):
            theta_copy(par, d).wait()
        total = TS[par, 0]
        for d in range(1, N):
            total = total + TS[par, d]
        total = total / columns
        return jnp.concatenate(
            [jnp.broadcast_to(total[:, g * width:g * width + 1], (8, 128)) for g in range(groups)], axis=0
        )

    class Both:
        def __init__(self, up_src, up_dst, down_src, down_dst, send, recv):
            self.up = pltpu.make_async_remote_copy(
                src_ref=up_src, dst_ref=up_dst, send_sem=send[0], recv_sem=recv[0],
                device_id=right, device_id_type=MESH)
            self.down = pltpu.make_async_remote_copy(
                src_ref=down_src, dst_ref=down_dst, send_sem=send[1], recv_sem=recv[1],
                device_id=left, device_id_type=MESH)

        def start(self):
            @pl.when(jnp.logical_not(last))
            def _():
                self.up.start()

            @pl.when(jnp.logical_not(first))
            def _():
                self.down.start()

        def wait(self):
            @pl.when(jnp.logical_not(last))
            def _():
                self.up.wait_send()
                self.down.wait_recv()

            @pl.when(jnp.logical_not(first))
            def _():
                self.down.wait_send()
                self.up.wait_recv()

    def pair(sems, i=None):
        return (sems.at[0], sems.at[1]) if i is None else (sems.at[i, 0], sems.at[i, 1])

    def fields_exchange():
        return Both(F.at[:, R], F.at[:, 0], F.at[:, 1], F.at[:, R + 1], pair(a_s), pair(a_r))

    def speed_exchange():
        return Both(U.at[R], U.at[0], U.at[1], U.at[R + 1], pair(b_s), pair(b_r))

    def rim_exchange(buf, h, i):
        return Both(
            buf.at[pl.ds(H + R - h, h)], buf.at[pl.ds(H - h, h)],
            buf.at[pl.ds(H, h)], buf.at[pl.ds(H + R, h)], pair(c_s, i), pair(c_r, i))

    own_state.wait()
    for d in range(1, L):
        state_copy(d).wait_send()
        state_landing(d).wait_recv()

    def start_row(row, total):
        for l in range(L):
            u = F[0, row + 1, l] + prof[0]
            v = F[1, row + 1, l]
            warm = F[3, row + 1, l] + prof[1]
            F[0, row + 1, l] = u
            F[3, row + 1, l] = warm
            disk_sums(row, l, u, v)
            total = total + warm
        return total

    total = lax.fori_loop(0, R, start_row, jnp.zeros((K, 128), jnp.float32))
    fields_exchange().start()
    send_theta(0, total)

    @pl.when(gx == 0)
    def _():
        for d in range(1, NL):
            planes_copy(d).wait_send()

        @pl.when(gy != 0)
        def _():
            planes_copy(0).wait_send()

    @pl.when(first)
    def _():
        own_planes.wait()
        for d in range(NL):
            for j in range(L):
                if d or j:
                    planes_landing(d, j).wait_recv()

    def tendency_row(row, carry):
        x = row + 1
        for l in range(L):
            cen, dx, dy, dz, lap = [], [], [], [], []
            for c in range(4):
                tiles = {i % L: F[c, x, i % L] for i in (l - 1, l, l + 1)}
                f = tiles[l]
                xm, xp = F[c, x - 1, l], F[c, x + 1, l]
                ym, yp = beside_y(tiles, l)
                km, kp = beside_k(f, c != 2)
                cen.append(f)
                dx.append(xp - xm)
                dy.append(yp - ym)
                dz.append(kp - km)
                lap.append((xp + xm) + (kp + km) + (yp + ym) - 6.0 * f)
            square = 2.0 * (dx[0] * dx[0] + dy[1] * dy[1] + dz[2] * dz[2])
            for shear in (dy[0] + dx[1], dz[0] + dx[2], dz[1] + dy[2]):
                square = square + shear * shear
            nu = VISCOSITY + (0.5 * SMAGORINSKY) * jnp.sqrt(square)
            half_u, half_v, half_w = 0.5 * cen[0], 0.5 * cen[1], 0.5 * cen[2]
            for c in range(4):
                visc = nu if c < 3 else nu * DIFFUSIVITY_RATIO
                tend = lap[c] * visc - (half_u * dx[c] + half_v * dy[c] + half_w * dz[c])
                if c < 2:
                    force = FO[c, l, pl.ds(row, 1), :]
                    tend = tend + jnp.where(in_band, jnp.broadcast_to(force, (K, 128)), 0.0)
                elif c == 2:
                    tend = tend + BUOYANCY * cen[3]
                new = cen[c] + TIME_STEP * tend
                if c == 0:
                    U[x, l] = new
                else:
                    G[c - 1, row, l] = new
        return carry

    def source_row(row, mean):
        x = row + 1
        tiles = [G[0, row, l] for l in range(L)]
        for l in range(L):
            vm, vp = beside_y(tiles, l)
            w = G[1, row, l] - (TIME_STEP * BUOYANCY) * mean
            G[1, row, l] = w
            wm, wp = beside_k(w, False)
            RR[row + H, l] = ((U[x + 1, l] - U[x - 1, l]) + (vp - vm) + (wp - wm)) * 0.5
        return mean

    def sweep_row(index, from_source, x):
        old = RR if from_source else PP.at[index - 1]
        tiles = [old[x, l] for l in range(L)]
        inside = jnp.logical_not((first & (x < H)) | (last & (x >= R + H)))
        keep = jnp.where(inside, 1.0 / 6.0, 0.0).astype(jnp.float32)
        for l in range(L):
            ym, yp = beside_y(tiles, l)
            km, kp = beside_k(tiles[l])
            around = (old[x + 1, l] + old[x - 1, l]) + (ym + yp) + (km + kp)
            if from_source:
                new = (around * (-1.0 / 6.0) - tiles[l]) * keep
            else:
                new = (around - RR[x, l]) * keep
            PP[index, x, l] = new

    def sweep(index, v):
        begin, count = H - (v - 1), R + 2 * (v - 1)

        def body(i, c):
            sweep_row(index, index == 0, begin + 2 * i)
            sweep_row(index, index == 0, begin + 2 * i + 1)
            return c

        lax.fori_loop(0, count // 2, body, 0)

    def finish_row(row, total):
        x = row + H
        p = PP.at[SWEEPS - 1]
        tiles = [p[x, l] for l in range(L)]
        for l in range(L):
            ym, yp = beside_y(tiles, l)
            km, kp = beside_k(tiles[l])
            u = U[row + 1, l] - 0.5 * (p[x + 1, l] - p[x - 1, l])
            v = G[0, row, l] - 0.5 * (yp - ym)
            F[0, row + 1, l] = u
            F[1, row + 1, l] = v
            F[2, row + 1, l] = G[1, row, l] - 0.5 * (kp - km)
            warm = G[2, row, l]
            F[3, row + 1, l] = warm
            disk_sums(row, l, u, v)
            total = total + warm
        return total

    def edge_rows(body, carry):
        return lax.fori_loop(0, 2, lambda i, c: body(i * (R - 1), c), carry)

    def inner_rows(body, carry):
        return lax.fori_loop(1, R - 1, body, carry) if R > 2 else carry

    def step(n, carry):
        par = lax.rem(n, 2)

        @pl.when(first)
        def _():
            plane = slot[n]
            for c in range(4):
                for l in range(L):
                    f = PL[plane, c, l]
                    if c in (0, 3):
                        f = f + prof[0 if c == 0 else 1]
                    F[c, 0, l] = f
                    if c == 0:
                        U[0, l] = f

        @pl.when(last)
        def _():
            for c in range(4):
                F[c, R + 1] = F[c, R]

        disk_forces()
        inner_rows(tendency_row, 0)
        fields_exchange().wait()
        edge_rows(tendency_row, 0)

        @pl.when(last)
        def _():
            U[R + 1] = U[R]

        speed_exchange().start()
        mean = mean_theta(par)
        inner_rows(source_row, mean)
        speed_exchange().wait()
        edge_rows(source_row, mean)

        rim_exchange(RR, H, 0).start()
        rim_exchange(RR, H, 0).wait()
        v = H
        used = 1
        for i in range(SWEEPS):
            if v == 0:
                h = min(H, SWEEPS + 1 - i)
                rim_exchange(PP.at[i - 1], h, used).start()
                rim_exchange(PP.at[i - 1], h, used).wait()
                used += 1
                v = h
            sweep(i, v)
            v -= 1
        if v == 0:
            rim_exchange(PP.at[SWEEPS - 1], 1, used).start()
            rim_exchange(PP.at[SWEEPS - 1], 1, used).wait()

        total = edge_rows(finish_row, jnp.zeros((K, 128), jnp.float32))

        @pl.when(n < STEPS - 1)
        def _():
            fields_exchange().start()

        total = inner_rows(finish_row, total)

        @pl.when(n < STEPS - 1)
        def _():
            send_theta(1 - par, total)

        return carry

    lax.fori_loop(0, STEPS, step, 0)

    def out_copy(d):
        peer = lax.rem(gy + d, L)
        return pltpu.make_async_remote_copy(
            src_ref=F.at[:, pl.ds(1, R), peer],
            dst_ref=out.at[0, :, pl.ds(q_me * R, R)],
            send_sem=o_s.at[d], recv_sem=o_r.at[d],
            device_id={"gy": peer}, device_id_type=MESH,
        )

    def out_landing(d):
        peer = lax.rem(gy + L - d, L)
        return pltpu.make_async_remote_copy(
            src_ref=F.at[:, pl.ds(1, R), peer],
            dst_ref=out.at[0, :, pl.ds(turned(gx, peer) * R, R)],
            send_sem=o_s.at[d], recv_sem=o_r.at[d],
            device_id={"gy": peer}, device_id_type=MESH,
        )

    for d in range(1, L):
        out_copy(d).start()
    own_out = pltpu.make_async_copy(
        F.at[:, pl.ds(1, R), gy], out.at[0, :, pl.ds(q_me * R, R)], loc.at[3]
    )
    own_out.start()
    own_out.wait()
    for d in range(1, L):
        out_copy(d).wait_send()
        out_landing(d).wait_recv()


def solution(mesh):
    NL, GX, L = mesh.shape["layout"], mesh.shape["gx"], mesh.shape["gy"]

    def local(state, planes, turbine_cell, active, yaw_sector, slot):
        rows, K, cols = state.shape[2:]
        R = rows // L
        H = min(R, SWEEPS + 1)
        N = GX * L
        turbines = active.shape[1]
        held = planes.shape[0]
        ids = turbine_cell[0, :, K // 2, :].reshape(L, R, cols)
        angle = (yaw_sector[0].astype(jnp.float32) - 3.5) * YAW_INCREMENT
        table = jnp.stack([jnp.cos(angle), jnp.sin(angle), active[0].astype(jnp.float32)])
        prof = jnp.broadcast_to(profiles(K)[:, :, None], (2, K, cols))
        smem = pl.BlockSpec(memory_space=pltpu.SMEM)
        vmem = pl.BlockSpec(memory_space=pltpu.VMEM)
        hbm = pl.BlockSpec(memory_space=pl.ANY)
        f32 = jnp.float32
        dma = pltpu.SemaphoreType.DMA
        return pl.pallas_call(
            functools.partial(
                kernel, NL, GX, L, R, K, H, turbines, held, float(rows * GX * cols * L)
            ),
            out_shape=jax.ShapeDtypeStruct(state.shape, f32),
            in_specs=[smem, smem, vmem, vmem, hbm, hbm],
            out_specs=hbm,
            scratch_shapes=[
                pltpu.VMEM((4, R + 2, L, K, cols), f32),
                pltpu.VMEM((3, R, L, K, cols), f32),
                pltpu.VMEM((R + 2, L, K, cols), f32),
                pltpu.VMEM((R + 2 * H, L, K, cols), f32),
                pltpu.VMEM((SWEEPS, R + 2 * H, L, K, cols), f32),
                pltpu.VMEM((held * NL, 4, L, K, cols), f32),
                pltpu.VMEM((L, R, cols), jnp.int32),
                pltpu.VMEM((2, L, R, cols), f32),
                pltpu.VMEM((5, L, R, cols), f32),
                pltpu.VMEM((2, N, 8, 128), f32),
                dma((L,)), dma((L,)), dma((L,)), dma((L,)),
                dma((NL,)), dma((NL, L)),
                dma((2,)), dma((2,)), dma((2,)), dma((2,)),
                dma((SWEEPS + 1, 2)), dma((SWEEPS + 1, 2)),
                dma((2, N)), dma((2, N)),
                dma((L,)), dma((L,)),
                dma((4,)),
            ],
            compiler_params=pltpu.CompilerParams(
                collective_id=0, has_side_effects=True, vmem_limit_bytes=40 * 1024 * 1024
            ),
        )(slot, table, prof, ids, state, planes)

    return jax.shard_map(
        local,
        mesh=mesh,
        in_specs=(
            P("layout", None, "gx", None, "gy"),
            P("layout", None, None, "gy"),
            P("layout", "gx", None, "gy"),
            P("layout", None),
            P("layout", None),
            P(),
        ),
        out_specs=P("layout", None, "gx", None, "gy"),
        check_vma=False,
    )
```

```python
import functools

import jax
import jax.numpy as jnp
from jax import lax
from jax.experimental import pallas as pl
from jax.experimental.pallas import tpu as pltpu
from jax.sharding import PartitionSpec as P

STEPS = 4
SWEEPS = 4
RADIUS = 5

TIME_STEP = 0.25
VISCOSITY = 0.02
SMAGORINSKY = 0.0289
DIFFUSIVITY_RATIO = 1.0 / 0.7
BUOYANCY = 0.5
THRUST_COEFF = 1.33
YAW_INCREMENT = 0.1
MESH = pl.DeviceIdType.MESH


def profiles(levels):
    height = (jnp.arange(levels).astype(jnp.float32) + 0.5) / levels
    return jnp.stack([height ** (1.0 / 7.0), 0.5 * height])


def kernel(
    NL, GX, L, R, K, H, turbines, held, columns,
    slot, table, prof, ids, state, planes,
    out,
    F, G, U, RR, PP, PL, ID, SU, NM, FO, TS, EA, EM, EB, EC, EL,
    i_s, i_r, p_s, p_r, a_s, a_r, b_s, b_r, c_s, c_r, t_s, t_r, loc,
):
    lay = lax.axis_index("layout")
    gx = lax.axis_index("gx")
    gy = lax.axis_index("gy")
    N = GX * L
    s = gx * L + gy
    first = gx == 0
    last = gx == GX - 1
    inner_end = jnp.logical_not(last)
    inner_start = jnp.logical_not(first)
    up_x, down_x = lax.rem(gx + 1, GX), lax.rem(gx + GX - 1, GX)
    up_y, down_y = lax.rem(gy + 1, L), lax.rem(gy + L - 1, L)
    blocks = R // 8

    def device_of(t):
        return {"gx": t // L, "gy": lax.rem(t, L)}

    barrier = pltpu.get_barrier_semaphore()
    for d in range(1, N):
        pl.semaphore_signal(barrier, inc=1, device_id=device_of(lax.rem(s + d, N)), device_id_type=MESH)

    @pl.when(first)
    def _():
        for d in range(1, NL):
            pl.semaphore_signal(
                barrier, inc=1, device_id={"layout": lax.rem(lay + d, NL)}, device_id_type=MESH
            )

    own_state = pltpu.make_async_copy(state.at[0], F.at[:, pl.ds(1, R)], loc.at[0])
    own_planes = pltpu.make_async_copy(planes, PL.at[pl.ds(lay * held, held)], loc.at[1])
    own_state.start()

    @pl.when(first)
    def _():
        own_planes.start()

    zero = jnp.zeros((2, K, 128), jnp.float32)
    for buf in [RR] + [PP.at[i] for i in range(SWEEPS)]:
        @pl.when(first)
        def _():
            def body(i, c):
                buf[i] = zero
                return c
            lax.fori_loop(0, H, body, 0)

        @pl.when(last)
        def _():
            def body(i, c):
                buf[R + H + i] = zero
                return c
            lax.fori_loop(0, H, body, 0)

    EA[0] = zero[0]
    EB[0] = zero[0]
    for i in range(blocks):
        EC[i] = zero[0]
    ID[0] = ids[...]

    pl.semaphore_wait(barrier, N - 1 + jnp.where(first, NL - 1, 0))

    class Exchange:
        def __init__(self, send, recv):
            self.send, self.recv, self.items = send, recv, []

        def add(self, src, dst, device, out_if=None, in_if=None):
            i = len(self.items)
            copy = pltpu.make_async_remote_copy(
                src_ref=src, dst_ref=dst, send_sem=self.send.at[i], recv_sem=self.recv.at[i],
                device_id=device, device_id_type=MESH)
            self.items.append((copy, out_if, in_if))
            return self

        def rows(self, up_src, up_dst, down_src, down_dst):
            self.add(up_src, up_dst, {"gx": up_x}, inner_end, inner_start)
            return self.add(down_src, down_dst, {"gx": down_x}, inner_start, inner_end)

        def span(self, src, dst_above, dst_below):
            self.add(src, dst_above, {"gy": up_y})
            return self.add(src, dst_below, {"gy": down_y})

        def start(self, which=slice(None)):
            for copy, out_if, _ in self.items[which]:
                if out_if is None:
                    copy.start()
                else:
                    pl.when(out_if)(copy.start)

        def wait(self):
            for copy, out_if, in_if in self.items:
                if out_if is None:
                    copy.wait_send()
                    copy.wait_recv()
                else:
                    pl.when(out_if)(copy.wait_send)
                    pl.when(in_if)(copy.wait_recv)

    def ids_exchange():
        return Exchange(i_s, i_r).span(ID.at[0], ID.at[1], ID.at[2])

    def fields_exchange():
        e = Exchange(a_s, a_r).rows(F.at[:, R], F.at[:, 0], F.at[:, 1], F.at[:, R + 1])
        return e.span(EA.at[0], EA.at[1], EA.at[2]).span(NM.at[0], NM.at[1], NM.at[2])

    def speed_exchange():
        e = Exchange(b_s, b_r).rows(U.at[R], U.at[0], U.at[1], U.at[R + 1])
        return e.span(EB.at[0], EB.at[1], EB.at[2])

    def source_exchange():
        e = Exchange(c_s, c_r).rows(
            RR.at[pl.ds(R, H), 0], RR.at[pl.ds(0, H), 0],
            RR.at[pl.ds(H, H), 0], RR.at[pl.ds(H + R, H), 0])
        e.span(EC, EL.at[0, pl.ds(1, blocks)], EL.at[1, pl.ds(1, blocks)])
        for side, to in ((0, up_y), (1, down_y)):
            e.add(EC.at[blocks - 1], EL.at[side, 0], {"gx": up_x, "gy": to}, inner_end, inner_start)
            e.add(EC.at[0], EL.at[side, blocks + 1], {"gx": down_x, "gy": to}, inner_start, inner_end)
        return e

    def planes_copy(d):
        return pltpu.make_async_remote_copy(
            src_ref=planes, dst_ref=PL.at[pl.ds(lay * held, held)],
            send_sem=p_s.at[d], recv_sem=p_r.at[d],
            device_id={"layout": lax.rem(lay + d, NL)}, device_id_type=MESH,
        )

    def planes_landing(d):
        source = lax.rem(lay + NL - d, NL)
        return pltpu.make_async_remote_copy(
            src_ref=planes, dst_ref=PL.at[pl.ds(source * held, held)],
            send_sem=p_s.at[d], recv_sem=p_r.at[d],
            device_id={"layout": source}, device_id_type=MESH,
        )

    ids_exchange().start()

    @pl.when(first)
    def _():
        for d in range(1, NL):
            planes_copy(d).start()

    lane = lax.broadcasted_iota(jnp.int32, (K, 128), 1)
    level = lax.broadcasted_iota(jnp.int32, (K, 128), 0)
    at_first, at_last = lane == 0, lane == 127
    at_floor, at_top = level == 0, level == K - 1
    low = K // 2 - RADIUS
    in_band = (level >= low) & (level <= low + 2 * RADIUS)

    def beside_y(f, rim):
        before = pltpu.roll(jnp.where(at_last, rim, f), 1, 1)
        after = pltpu.roll(jnp.where(at_first, rim, f), 127, 1)
        return before, after

    def beside_k(f, keep=True):
        edge = f if keep else jnp.zeros_like(f)
        below = jnp.where(at_floor, edge, pltpu.roll(f, 1, 0))
        above = jnp.where(at_top, edge, pltpu.roll(f, K - 1, 0))
        return below, above

    def pack(packed, f, j, width):
        return jnp.where(lane // width == j, pltpu.roll(f, width * j + width // 2, 1), packed)

    def unpack(packed, j, width):
        return pltpu.roll(packed, 128 - width // 2 - width * j, 1)

    own_ids = ID[0]
    cosines = jnp.zeros((R, 128), jnp.float32)
    sines, runs = cosines, cosines
    for t in range(turbines):
        here = own_ids == t
        cosines = jnp.where(here, table[0, t], cosines)
        sines = jnp.where(here, table[1, t], sines)
        runs = jnp.where(here, table[2, t], runs)
    FO[2] = cosines
    FO[3] = sines
    FO[4] = runs

    def disk_forces():
        lane_r = lax.broadcasted_iota(jnp.int32, (R, 128), 1)
        names = [ID[i] for i in range(3)]
        normal = [NM[i] for i in range(3)]
        total = normal[0]
        for shift in range(1, 2 * RADIUS + 1):
            for other, amount, wraps in (
                (1, shift, lane_r >= 128 - shift), (2, 128 - shift, lane_r < shift)
            ):
                n_sh = pltpu.roll(jnp.where(wraps, normal[other], normal[0]), amount, 1)
                i_sh = pltpu.roll(jnp.where(wraps, names[other], names[0]), amount, 1)
                total = total + jnp.where(i_sh == names[0], n_sh, 0.0)
        speed = total / float((2 * RADIUS + 1) ** 2)
        thrust = -0.5 * THRUST_COEFF * speed * jnp.abs(speed) * FO[4]
        FO[0] = thrust * FO[2]
        FO[1] = thrust * FO[3]

    def disk_sums(row, u, v):
        SU[0, pl.ds(row, 1), :] = jnp.sum(jnp.where(in_band, u, 0.0), axis=0, keepdims=True)
        SU[1, pl.ds(row, 1), :] = jnp.sum(jnp.where(in_band, v, 0.0), axis=0, keepdims=True)

    def send_span():
        NM[0] = SU[0] * FO[2] + SU[1] * FO[3]
        fields_exchange().start(slice(2, None))

    groups = K // 8
    width = 128 // groups
    lane_8 = lax.broadcasted_iota(jnp.int32, (8, 128), 1)

    def theta_copy(par, d):
        return pltpu.make_async_remote_copy(
            src_ref=TS.at[par, 0], dst_ref=TS.at[par, d],
            send_sem=t_s.at[par, d], recv_sem=t_r.at[par, d],
            device_id=device_of(lax.rem(s + d, N)), device_id_type=MESH,
        )

    def send_theta(par, total):
        packed = jnp.zeros((8, 128), jnp.float32)
        for g in range(groups):
            part = jnp.sum(total[g * 8:(g + 1) * 8], axis=1, keepdims=True)
            packed = jnp.where(lane_8 // width == g, part, packed)
        TS[par, 0] = packed
        for d in range(1, N):
            theta_copy(par, d).start()

    def mean_theta(par):
        for d in range(1, N):
            theta_copy(par, d).wait()
        total = TS[par, 0]
        for d in range(1, N):
            total = total + TS[par, d]
        total = total / columns
        return jnp.concatenate(
            [jnp.broadcast_to(total[:, g * width:g * width + 1], (8, 128)) for g in range(groups)], axis=0
        )

    own_state.wait()

    def start_row(row, total):
        u = F[0, row + 1] + prof[0]
        v = F[1, row + 1]
        warm = F[3, row + 1] + prof[1]
        F[0, row + 1] = u
        F[3, row + 1] = warm
        disk_sums(row, u, v)
        packed = EA[0]
        for c, f in enumerate((u, v, F[2, row + 1], warm)):
            packed = pack(packed, f, c * R + row, 2)
        EA[0] = packed
        return total + warm

    total = lax.fori_loop(0, R, start_row, jnp.zeros((K, 128), jnp.float32))
    fields_exchange().start(slice(0, 2))
    send_span()
    send_theta(0, total)
    ids_exchange().wait()

    @pl.when(first)
    def _():
        own_planes.wait()
        for d in range(1, NL):
            planes_copy(d).wait_send()
            planes_landing(d).wait_recv()

    def tendency_row(row, carry):
        x = row + 1
        rims = EM[...]
        cen, dx, dy, dz, lap = [], [], [], [], []
        for c in range(4):
            f = F[c, x]
            xm, xp = F[c, x - 1], F[c, x + 1]
            ym, yp = beside_y(f, unpack(rims, c * R + row, 2))
            km, kp = beside_k(f, c != 2)
            cen.append(f)
            dx.append(xp - xm)
            dy.append(yp - ym)
            dz.append(kp - km)
            lap.append((xp + xm) + (kp + km) + (yp + ym) - 6.0 * f)
        square = 2.0 * (dx[0] * dx[0] + dy[1] * dy[1] + dz[2] * dz[2])
        for shear in (dy[0] + dx[1], dz[0] + dx[2], dz[1] + dy[2]):
            square = square + shear * shear
        nu = VISCOSITY + (0.5 * SMAGORINSKY) * jnp.sqrt(square)
        half_u, half_v, half_w = 0.5 * cen[0], 0.5 * cen[1], 0.5 * cen[2]
        for c in range(4):
            visc = nu if c < 3 else nu * DIFFUSIVITY_RATIO
            tend = lap[c] * visc - (half_u * dx[c] + half_v * dy[c] + half_w * dz[c])
            if c < 2:
                force = FO[c, pl.ds(row, 1), :]
                tend = tend + jnp.where(in_band, jnp.broadcast_to(force, (K, 128)), 0.0)
            elif c == 2:
                tend = tend + BUOYANCY * cen[3]
            new = cen[c] + TIME_STEP * tend
            if c == 0:
                U[x] = new
            else:
                G[c - 1, row] = new
            if c == 1:
                EB[0] = pack(EB[0], new, row, 2)
        return carry

    def source_row(row, mean):
        x = row + 1
        vm, vp = beside_y(G[0, row], unpack(EM[...], row, 2))
        w = G[1, row] - (TIME_STEP * BUOYANCY) * mean
        G[1, row] = w
        wm, wp = beside_k(w, False)
        r = ((U[x + 1] - U[x - 1]) + (vp - vm) + (wp - wm)) * 0.5
        RR[row + H, 0] = r
        EC[row // 8] = pack(EC[row // 8], r, lax.rem(row, 8), 16)
        return mean

    def rim_row(x, carry):
        shifted = x - H + 8
        b = shifted // 8
        merged = jnp.where(lax.rem(lane, 16) >= 8, EL[1, b], EL[0, b])
        RR[x, 1] = unpack(merged, lax.rem(shifted, 8), 16)
        return carry

    def sweep_row(index, x):
        old = RR if index == 0 else PP.at[index - 1]
        tiles = [old[x, l] for l in range(2)]
        inside = jnp.logical_not((first & (x < H)) | (last & (x >= R + H)))
        keep = jnp.where(inside, 1.0 / 6.0, 0.0).astype(jnp.float32)
        for l in range(2):
            ym, yp = beside_y(tiles[l], tiles[1 - l])
            km, kp = beside_k(tiles[l])
            around = (old[x + 1, l] + old[x - 1, l]) + (ym + yp) + (km + kp)
            if index == 0:
                new = (around * (-1.0 / 6.0) - tiles[l]) * keep
            else:
                new = (around - RR[x, l]) * keep
            PP[index, x, l] = new

    def sweep(index, v):
        begin, count = H - (v - 1), R + 2 * (v - 1)

        def body(i, c):
            sweep_row(index, begin + 2 * i)
            sweep_row(index, begin + 2 * i + 1)
            return c

        lax.fori_loop(0, count // 2, body, 0)

    def finish_row(row, total):
        x = row + H
        p = PP.at[SWEEPS - 1]
        centre = p[x, 0]
        ym, yp = beside_y(centre, p[x, 1])
        km, kp = beside_k(centre)
        u = U[row + 1] - 0.5 * (p[x + 1, 0] - p[x - 1, 0])
        v = G[0, row] - 0.5 * (yp - ym)
        w = G[1, row] - 0.5 * (kp - km)
        warm = G[2, row]
        disk_sums(row, u, v)
        packed = EA[0]
        for c, f in enumerate((u, v, w, warm)):
            F[c, row + 1] = f
            packed = pack(packed, f, c * R + row, 2)
        EA[0] = packed
        return total + warm

    def edge_rows(body, carry):
        return lax.fori_loop(0, 2, lambda i, c: body(i * (R - 1), c), carry)

    def inner_rows(body, carry):
        return lax.fori_loop(1, R - 1, body, carry)

    odd_lane = lax.rem(lane, 2) == 1

    def step(n, carry):
        par = lax.rem(n, 2)

        @pl.when(first)
        def _():
            plane = slot[n]
            for c in range(4):
                f = PL[plane, c]
                if c in (0, 3):
                    f = f + prof[0 if c == 0 else 1]
                F[c, 0] = f
                if c == 0:
                    U[0] = f

        @pl.when(last)
        def _():
            for c in range(4):
                F[c, R + 1] = F[c, R]

        fields_exchange().wait()
        EM[...] = jnp.where(odd_lane, EA[2], EA[1])
        disk_forces()
        lax.fori_loop(0, R, tendency_row, 0)

        @pl.when(last)
        def _():
            U[R + 1] = U[R]

        speed_exchange().start()
        mean = mean_theta(par)
        speed_exchange().wait()
        EM[...] = jnp.where(odd_lane, EB[2], EB[1])
        lax.fori_loop(0, R, source_row, mean)

        source_exchange().start()
        source_exchange().wait()
        lax.fori_loop(jnp.where(first, H, 0), jnp.where(last, R + H, R + 2 * H), rim_row, 0)
        for i in range(SWEEPS):
            sweep(i, H - i)

        total = edge_rows(finish_row, jnp.zeros((K, 128), jnp.float32))

        @pl.when(n < STEPS - 1)
        def _():
            fields_exchange().start(slice(0, 2))

        total = inner_rows(finish_row, total)

        @pl.when(n < STEPS - 1)
        def _():
            send_span()
            send_theta(1 - par, total)

        return carry

    lax.fori_loop(0, STEPS, step, 0)

    own_out = pltpu.make_async_copy(F.at[:, pl.ds(1, R)], out.at[0], loc.at[2])
    own_out.start()
    own_out.wait()


def solution(mesh):
    NL, GX, L = mesh.shape["layout"], mesh.shape["gx"], mesh.shape["gy"]

    def local(state, planes, turbine_cell, active, yaw_sector, slot):
        rows, K, cols = state.shape[2:]
        R = rows
        H = SWEEPS + 1
        N = GX * L
        turbines = active.shape[1]
        held = planes.shape[0]
        ids = turbine_cell[0, :, K // 2, :]
        angle = (yaw_sector[0].astype(jnp.float32) - 3.5) * YAW_INCREMENT
        table = jnp.stack([jnp.cos(angle), jnp.sin(angle), active[0].astype(jnp.float32)])
        prof = jnp.broadcast_to(profiles(K)[:, :, None], (2, K, cols))
        smem = pl.BlockSpec(memory_space=pltpu.SMEM)
        vmem = pl.BlockSpec(memory_space=pltpu.VMEM)
        hbm = pl.BlockSpec(memory_space=pl.ANY)
        f32 = jnp.float32
        dma = pltpu.SemaphoreType.DMA
        return pl.pallas_call(
            functools.partial(
                kernel, NL, GX, L, R, K, H, turbines, held, float(rows * GX * cols * L)
            ),
            out_shape=jax.ShapeDtypeStruct(state.shape, f32),
            in_specs=[smem, smem, vmem, vmem, hbm, hbm],
            out_specs=hbm,
            scratch_shapes=[
                pltpu.VMEM((4, R + 2, K, cols), f32),
                pltpu.VMEM((3, R, K, cols), f32),
                pltpu.VMEM((R + 2, K, cols), f32),
                pltpu.VMEM((R + 2 * H, 2, K, cols), f32),
                pltpu.VMEM((SWEEPS, R + 2 * H, 2, K, cols), f32),
                pltpu.VMEM((held * NL, 4, K, cols), f32),
                pltpu.VMEM((3, R, cols), jnp.int32),
                pltpu.VMEM((2, R, cols), f32),
                pltpu.VMEM((3, R, cols), f32),
                pltpu.VMEM((5, R, cols), f32),
                pltpu.VMEM((2, N, 8, 128), f32),
                pltpu.VMEM((3, K, cols), f32),
                pltpu.VMEM((K, cols), f32),
                pltpu.VMEM((3, K, cols), f32),
                pltpu.VMEM((R // 8, K, cols), f32),
                pltpu.VMEM((2, R // 8 + 2, K, cols), f32),
                dma((2,)), dma((2,)), dma((NL,)), dma((NL,)),
                dma((6,)), dma((6,)), dma((4,)), dma((4,)), dma((8,)), dma((8,)),
                dma((2, N)), dma((2, N)),
                dma((3,)),
            ],
            compiler_params=pltpu.CompilerParams(
                collective_id=0, has_side_effects=True, vmem_limit_bytes=40 * 1024 * 1024
            ),
        )(slot, table, prof, ids, state, planes)

    return jax.shard_map(
        local,
        mesh=mesh,
        in_specs=(
            P("layout", None, "gx", None, "gy"),
            P("layout", None, None, "gy"),
            P("layout", "gx", None, "gy"),
            P("layout", None),
            P("layout", None),
            P(),
        ),
        out_specs=P("layout", None, "gx", None, "gy"),
        check_vma=False,
    )
```

```python
import functools

import jax
import jax.numpy as jnp
from jax import lax
from jax.experimental import pallas as pl
from jax.experimental.pallas import tpu as pltpu
from jax.sharding import PartitionSpec as P

STEPS = 4
SWEEPS = 4
RADIUS = 5

TIME_STEP = 0.25
VISCOSITY = 0.02
SMAGORINSKY = 0.0289
DIFFUSIVITY_RATIO = 1.0 / 0.7
BUOYANCY = 0.5
THRUST_COEFF = 1.33
YAW_INCREMENT = 0.1
MESH = pl.DeviceIdType.MESH


def profiles(levels):
    height = (jnp.arange(levels).astype(jnp.float32) + 0.5) / levels
    return jnp.stack([height ** (1.0 / 7.0), 0.5 * height])


def kernel(
    NL, GX, L, R, K, H, turbines, held, columns,
    slot, table, prof, ids, state, planes,
    out,
    F, G, U, RR, P0, P1, P2, P3, PL, ID, SU, NM, FO, TS, EA, EM, EB, EC, EL,
    i_s, i_r, p_s, p_r, a_s, a_r, b_s, b_r, c_s, c_r, t_s, t_r, loc,
):
    lay = lax.axis_index("layout")
    gx = lax.axis_index("gx")
    gy = lax.axis_index("gy")
    N = GX * L
    s = gx * L + gy
    first = gx == 0
    last = gx == GX - 1
    inner_end = jnp.logical_not(last)
    inner_start = jnp.logical_not(first)
    up_x, down_x = lax.rem(gx + 1, GX), lax.rem(gx + GX - 1, GX)
    up_y, down_y = lax.rem(gy + 1, L), lax.rem(gy + L - 1, L)
    blocks = R // 8
    PP = [P0, P1, P2, P3]

    def device_of(t):
        return {"gx": t // L, "gy": lax.rem(t, L)}

    barrier = pltpu.get_barrier_semaphore()
    for d in range(1, N):
        pl.semaphore_signal(barrier, inc=1, device_id=device_of(lax.rem(s + d, N)), device_id_type=MESH)

    @pl.when(first)
    def _():
        for d in range(1, NL):
            pl.semaphore_signal(
                barrier, inc=1, device_id={"layout": lax.rem(lay + d, NL)}, device_id_type=MESH
            )

    own_state = pltpu.make_async_copy(state.at[0], F.at[:, pl.ds(1, R)], loc.at[0])
    own_planes = pltpu.make_async_copy(planes, PL.at[pl.ds(lay * held, held)], loc.at[1])
    own_state.start()

    @pl.when(first)
    def _():
        own_planes.start()

    zero = jnp.zeros((2, K, 128), jnp.float32)
    for buf in [RR] + PP:
        @pl.when(first)
        def _():
            def body(i, c):
                buf[i] = zero
                return c
            lax.fori_loop(0, H, body, 0)

        @pl.when(last)
        def _():
            def body(i, c):
                buf[R + H + i] = zero
                return c
            lax.fori_loop(0, H, body, 0)

    ID[0] = ids[...]

    pl.semaphore_wait(barrier, N - 1 + jnp.where(first, NL - 1, 0))

    class Exchange:
        def __init__(self, send, recv):
            self.send, self.recv, self.items = send, recv, []

        def add(self, src, dst, device, out_if=None, in_if=None):
            i = len(self.items)

            def copy():
                return pltpu.make_async_remote_copy(
                    src_ref=src, dst_ref=dst, send_sem=self.send.at[i], recv_sem=self.recv.at[i],
                    device_id=device, device_id_type=MESH)

            self.items.append((copy, out_if, in_if))
            return self

        def rows(self, up_src, up_dst, down_src, down_dst):
            self.add(up_src, up_dst, {"gx": up_x}, inner_end, inner_start)
            return self.add(down_src, down_dst, {"gx": down_x}, inner_start, inner_end)

        def span(self, src, dst_above, dst_below):
            self.add(src, dst_above, {"gy": up_y})
            return self.add(src, dst_below, {"gy": down_y})

        def start(self, which=slice(None)):
            for copy, out_if, _ in self.items[which]:
                if out_if is None:
                    copy().start()
                else:
                    pl.when(out_if)(lambda: copy().start())

        def wait(self):
            for copy, out_if, in_if in self.items:
                if out_if is None:
                    copy().wait()
                else:
                    pl.when(out_if)(lambda: copy().wait_send())
                    pl.when(in_if)(lambda: copy().wait_recv())

    def ids_exchange():
        return Exchange(i_s, i_r).span(ID.at[0], ID.at[1], ID.at[2])

    def fields_exchange():
        e = Exchange(a_s, a_r).rows(F.at[:, R], F.at[:, 0], F.at[:, 1], F.at[:, R + 1])
        return e.span(EA.at[0], EA.at[1], EA.at[2]).span(NM.at[0], NM.at[1], NM.at[2])

    def speed_exchange():
        e = Exchange(b_s, b_r).rows(U.at[R], U.at[0], U.at[1], U.at[R + 1])
        return e.span(EB.at[0], EB.at[1], EB.at[2])

    def source_exchange():
        e = Exchange(c_s, c_r).rows(
            RR.at[pl.ds(R, H), 0], RR.at[pl.ds(0, H), 0],
            RR.at[pl.ds(H, H), 0], RR.at[pl.ds(H + R, H), 0])
        e.span(EC, EL.at[0, pl.ds(1, blocks)], EL.at[1, pl.ds(1, blocks)])
        for side, to in ((0, up_y), (1, down_y)):
            e.add(EC.at[blocks - 1], EL.at[side, 0], {"gx": up_x, "gy": to}, inner_end, inner_start)
            e.add(EC.at[0], EL.at[side, blocks + 1], {"gx": down_x, "gy": to}, inner_start, inner_end)
        return e

    def planes_copy(d):
        return pltpu.make_async_remote_copy(
            src_ref=planes, dst_ref=PL.at[pl.ds(lay * held, held)],
            send_sem=p_s.at[d], recv_sem=p_r.at[d],
            device_id={"layout": lax.rem(lay + d, NL)}, device_id_type=MESH,
        )

    def planes_landing(d):
        source = lax.rem(lay + NL - d, NL)
        return pltpu.make_async_remote_copy(
            src_ref=planes, dst_ref=PL.at[pl.ds(source * held, held)],
            send_sem=p_s.at[d], recv_sem=p_r.at[d],
            device_id={"layout": source}, device_id_type=MESH,
        )

    ids_exchange().start()

    @pl.when(first)
    def _():
        for d in range(1, NL):
            planes_copy(d).start()

    lane = lax.broadcasted_iota(jnp.int32, (K, 128), 1)
    level = lax.broadcasted_iota(jnp.int32, (K, 128), 0)
    at_first, at_last = lane == 0, lane == 127
    odd_lane = lax.rem(lane, 2) == 1
    at_floor, at_top = level == 0, level == K - 1
    low = K // 2 - RADIUS
    in_band = (level >= low) & (level <= low + 2 * RADIUS)

    def beside_y(f, rim):
        before = pltpu.roll(jnp.where(at_last, rim, f), 1, 1)
        after = pltpu.roll(jnp.where(at_first, rim, f), 127, 1)
        return before, after

    def beside_k(f, keep=True):
        edge = f if keep else jnp.zeros_like(f)
        below = jnp.where(at_floor, edge, pltpu.roll(f, 1, 0))
        above = jnp.where(at_top, edge, pltpu.roll(f, K - 1, 0))
        return below, above

    def pack(packed, f, j, width):
        return jnp.where(lane // width == j, pltpu.roll(f, width * j + width // 2, 1), packed)

    def unpack(packed, j, width):
        return pltpu.roll(packed, 128 - width // 2 - width * j, 1)

    own_ids = ID[0]
    cosines = jnp.zeros((R, 128), jnp.float32)
    sines, runs = cosines, cosines
    for t in range(turbines):
        here = own_ids == t
        cosines = jnp.where(here, table[0, t], cosines)
        sines = jnp.where(here, table[1, t], sines)
        runs = jnp.where(here, table[2, t], runs)
    FO[2] = cosines
    FO[3] = sines
    FO[4] = runs

    def disk_forces():
        lane_r = lax.broadcasted_iota(jnp.int32, (R, 128), 1)
        names = [ID[i] for i in range(3)]
        normal = [NM[i] for i in range(3)]
        total = normal[0]
        for shift in range(1, 2 * RADIUS + 1):
            for other, amount, wraps in (
                (1, shift, lane_r >= 128 - shift), (2, 128 - shift, lane_r < shift)
            ):
                n_sh = pltpu.roll(jnp.where(wraps, normal[other], normal[0]), amount, 1)
                i_sh = pltpu.roll(jnp.where(wraps, names[other], names[0]), amount, 1)
                total = total + jnp.where(i_sh == names[0], n_sh, 0.0)
        speed = total / float((2 * RADIUS + 1) ** 2)
        thrust = -0.5 * THRUST_COEFF * speed * jnp.abs(speed) * FO[4]
        FO[0] = thrust * FO[2]
        FO[1] = thrust * FO[3]

    def disk_sums(row, u, v):
        SU[0, row:row + 1, :] = jnp.sum(jnp.where(in_band, u, 0.0), axis=0, keepdims=True)
        SU[1, row:row + 1, :] = jnp.sum(jnp.where(in_band, v, 0.0), axis=0, keepdims=True)

    def send_span():
        NM[0] = SU[0] * FO[2] + SU[1] * FO[3]
        fields_exchange().start(slice(2, None))

    groups = K // 8
    width = 128 // groups
    lane_8 = lax.broadcasted_iota(jnp.int32, (8, 128), 1)

    def theta_copy(par, d):
        return pltpu.make_async_remote_copy(
            src_ref=TS.at[par, 0], dst_ref=TS.at[par, d],
            send_sem=t_s.at[par, d], recv_sem=t_r.at[par, d],
            device_id=device_of(lax.rem(s + d, N)), device_id_type=MESH,
        )

    def send_theta(par, total):
        packed = jnp.zeros((8, 128), jnp.float32)
        for g in range(groups):
            part = jnp.sum(total[g * 8:(g + 1) * 8], axis=1, keepdims=True)
            packed = jnp.where(lane_8 // width == g, part, packed)
        TS[par, 0] = packed
        for d in range(1, N):
            theta_copy(par, d).start()

    def mean_theta(par):
        for d in range(1, N):
            theta_copy(par, d).wait()
        total = TS[par, 0]
        for d in range(1, N):
            total = total + TS[par, d]
        total = total / columns
        return jnp.concatenate(
            [jnp.broadcast_to(total[:, g * width:g * width + 1], (8, 128)) for g in range(groups)], axis=0
        )

    own_state.wait()

    total = jnp.zeros((K, 128), jnp.float32)
    packed = zero[0]
    for row in range(R):
        u = F[0, row + 1] + prof[0]
        v = F[1, row + 1]
        warm = F[3, row + 1] + prof[1]
        F[0, row + 1] = u
        F[3, row + 1] = warm
        disk_sums(row, u, v)
        for c, f in enumerate((u, v, F[2, row + 1], warm)):
            packed = pack(packed, f, c * R + row, 2)
        total = total + warm
    EA[0] = packed
    fields_exchange().start(slice(0, 2))
    send_span()
    send_theta(0, total)
    ids_exchange().wait()

    @pl.when(first)
    def _():
        own_planes.wait()
        for d in range(1, NL):
            planes_copy(d).wait_send()
            planes_landing(d).wait_recv()

    def tendency_row(row, carry):
        x = row + 1
        rims = EM[...]
        cen, dx, dy, dz, lap = [], [], [], [], []
        for c in range(4):
            f = F[c, x]
            xm, xp = F[c, x - 1], F[c, x + 1]
            ym, yp = beside_y(f, unpack(rims, c * R + row, 2))
            km, kp = beside_k(f, c != 2)
            cen.append(f)
            dx.append(xp - xm)
            dy.append(yp - ym)
            dz.append(kp - km)
            lap.append((xp + xm) + (kp + km) + (yp + ym) - 6.0 * f)
        square = 2.0 * (dx[0] * dx[0] + dy[1] * dy[1] + dz[2] * dz[2])
        for shear in (dy[0] + dx[1], dz[0] + dx[2], dz[1] + dy[2]):
            square = square + shear * shear
        nu = VISCOSITY + (0.5 * SMAGORINSKY) * jnp.sqrt(square)
        half_u, half_v, half_w = 0.5 * cen[0], 0.5 * cen[1], 0.5 * cen[2]
        for c in range(4):
            visc = nu if c < 3 else nu * DIFFUSIVITY_RATIO
            tend = lap[c] * visc - (half_u * dx[c] + half_v * dy[c] + half_w * dz[c])
            if c < 2:
                force = FO[c, pl.ds(row, 1), :]
                tend = tend + jnp.where(in_band, jnp.broadcast_to(force, (K, 128)), 0.0)
            elif c == 2:
                tend = tend + BUOYANCY * cen[3]
            new = cen[c] + TIME_STEP * tend
            if c == 0:
                U[x] = new
            else:
                G[c - 1, row] = new
        return carry

    def pack_speed():
        packed = zero[0]
        for row in range(R):
            packed = pack(packed, G[0, row], row, 2)
        EB[0] = packed

    def sources(mean):
        rims = jnp.where(odd_lane, EB[2], EB[1])
        lift = (TIME_STEP * BUOYANCY) * mean
        for b in range(blocks):
            packed = zero[0]
            for j in range(8):
                row = 8 * b + j
                vm, vp = beside_y(G[0, row], unpack(rims, row, 2))
                w = G[1, row] - lift
                G[1, row] = w
                wm, wp = beside_k(w, False)
                r = ((U[row + 2] - U[row]) + (vp - vm) + (wp - wm)) * 0.5
                RR[row + H, 0] = r
                packed = pack(packed, r, j, 16)
            EC[b] = packed

    def rims():
        right_half = lax.rem(lane, 16) >= 8

        def block(b, items):
            merged = jnp.where(right_half, EL[1, b], EL[0, b])
            for j in items:
                RR[8 * (b - 1) + j + H, 1] = unpack(merged, j, 16)

        pl.when(inner_start)(lambda: block(0, range(8 - H, 8)))
        for b in range(1, blocks + 1):
            block(b, range(8))
        pl.when(inner_end)(lambda: block(blocks + 1, range(H)))

    def sweep(index, v):
        old = RR if index == 0 else PP[index - 1]
        sixth = jnp.float32(1.0 / 6.0)
        at_start = jnp.where(first, 0.0, sixth).astype(jnp.float32)
        at_end = jnp.where(last, 0.0, sixth).astype(jnp.float32)
        for x in range(H - (v - 1), R + H + (v - 1)):
            keep = at_start if x < H else at_end if x >= R + H else sixth
            tiles = [old[x, l] for l in range(2)]
            for l in range(2):
                ym, yp = beside_y(tiles[l], tiles[1 - l])
                km, kp = beside_k(tiles[l])
                around = (old[x + 1, l] + old[x - 1, l]) + (ym + yp) + (km + kp)
                if index == 0:
                    new = (around * (-1.0 / 6.0) - tiles[l]) * keep
                else:
                    new = (around - RR[x, l]) * keep
                PP[index][x, l] = new

    def finish():
        p = PP[SWEEPS - 1]
        total = zero[0]
        packed = zero[0]
        for row in range(R):
            x = row + H
            centre = p[x, 0]
            ym, yp = beside_y(centre, p[x, 1])
            km, kp = beside_k(centre)
            u = U[row + 1] - 0.5 * (p[x + 1, 0] - p[x - 1, 0])
            v = G[0, row] - 0.5 * (yp - ym)
            w = G[1, row] - 0.5 * (kp - km)
            warm = G[2, row]
            disk_sums(row, u, v)
            for c, f in enumerate((u, v, w, warm)):
                F[c, row + 1] = f
                packed = pack(packed, f, c * R + row, 2)
            total = total + warm
        EA[0] = packed
        return total

    def step(n, carry):
        par = lax.rem(n, 2)

        @pl.when(first)
        def _():
            plane = slot[n]
            for c in range(4):
                f = PL[plane, c]
                if c in (0, 3):
                    f = f + prof[0 if c == 0 else 1]
                F[c, 0] = f
                if c == 0:
                    U[0] = f

        @pl.when(last)
        def _():
            for c in range(4):
                F[c, R + 1] = F[c, R]

        fields_exchange().wait()
        EM[...] = jnp.where(odd_lane, EA[2], EA[1])
        disk_forces()
        lax.fori_loop(0, R // 2, lambda i, c: tendency_row(2 * i + 1, tendency_row(2 * i, c)), 0)
        pack_speed()

        @pl.when(last)
        def _():
            U[R + 1] = U[R]

        speed_exchange().start()
        mean = mean_theta(par)
        speed_exchange().wait()
        sources(mean)

        source_exchange().start()
        source_exchange().wait()
        rims()
        for i in range(SWEEPS):
            sweep(i, H - i)

        total = finish()

        @pl.when(n < STEPS - 1)
        def _():
            fields_exchange().start(slice(0, 2))
            send_span()
            send_theta(1 - par, total)

        return carry

    lax.fori_loop(0, STEPS, step, 0)

    own_out = pltpu.make_async_copy(F.at[:, pl.ds(1, R)], out.at[0], loc.at[2])
    own_out.start()
    own_out.wait()


def solution(mesh):
    NL, GX, L = mesh.shape["layout"], mesh.shape["gx"], mesh.shape["gy"]

    def local(state, planes, turbine_cell, active, yaw_sector, slot):
        rows, K, cols = state.shape[2:]
        R = rows
        H = SWEEPS + 1
        N = GX * L
        turbines = active.shape[1]
        held = planes.shape[0]
        ids = turbine_cell[0, :, K // 2, :]
        angle = (yaw_sector[0].astype(jnp.float32) - 3.5) * YAW_INCREMENT
        table = jnp.stack([jnp.cos(angle), jnp.sin(angle), active[0].astype(jnp.float32)])
        prof = jnp.broadcast_to(profiles(K)[:, :, None], (2, K, cols))
        smem = pl.BlockSpec(memory_space=pltpu.SMEM)
        vmem = pl.BlockSpec(memory_space=pltpu.VMEM)
        hbm = pl.BlockSpec(memory_space=pl.ANY)
        f32 = jnp.float32
        dma = pltpu.SemaphoreType.DMA
        return pl.pallas_call(
            functools.partial(
                kernel, NL, GX, L, R, K, H, turbines, held, float(rows * GX * cols * L)
            ),
            out_shape=jax.ShapeDtypeStruct(state.shape, f32),
            in_specs=[smem, smem, vmem, vmem, hbm, hbm],
            out_specs=hbm,
            scratch_shapes=[
                pltpu.VMEM((4, R + 2, K, cols), f32),
                pltpu.VMEM((3, R, K, cols), f32),
                pltpu.VMEM((R + 2, K, cols), f32),
                pltpu.VMEM((R + 2 * H, 2, K, cols), f32),
                pltpu.VMEM((R + 2 * H, 2, K, cols), f32),
                pltpu.VMEM((R + 2 * H, 2, K, cols), f32),
                pltpu.VMEM((R + 2 * H, 2, K, cols), f32),
                pltpu.VMEM((R + 2 * H, 2, K, cols), f32),
                pltpu.VMEM((held * NL, 4, K, cols), f32),
                pltpu.VMEM((3, R, cols), jnp.int32),
                pltpu.VMEM((2, R, cols), f32),
                pltpu.VMEM((3, R, cols), f32),
                pltpu.VMEM((5, R, cols), f32),
                pltpu.VMEM((2, N, 8, 128), f32),
                pltpu.VMEM((3, K, cols), f32),
                pltpu.VMEM((K, cols), f32),
                pltpu.VMEM((3, K, cols), f32),
                pltpu.VMEM((R // 8, K, cols), f32),
                pltpu.VMEM((2, R // 8 + 2, K, cols), f32),
                dma((2,)), dma((2,)), dma((NL,)), dma((NL,)),
                dma((6,)), dma((6,)), dma((4,)), dma((4,)), dma((8,)), dma((8,)),
                dma((2, N)), dma((2, N)),
                dma((3,)),
            ],
            compiler_params=pltpu.CompilerParams(
                collective_id=0, has_side_effects=True, vmem_limit_bytes=40 * 1024 * 1024
            ),
        )(slot, table, prof, ids, state, planes)

    return jax.shard_map(
        local,
        mesh=mesh,
        in_specs=(
            P("layout", None, "gx", None, "gy"),
            P("layout", None, None, "gy"),
            P("layout", "gx", None, "gy"),
            P("layout", None),
            P("layout", None),
            P(),
        ),
        out_specs=P("layout", None, "gx", None, "gy"),
        check_vma=False,
    )
```
